512 devices in a mesh: dp: 8 (over y), pipe: 4 (over z_lo), tensor: 16 (over z_hi, x, core).
Axes of the slice: x: 4, y: 8, z: 8 (z_hi: 2, z_lo: 4; z = z_hi * 4 + z_lo), core: 2. Of those that a mesh axis runs over, the one named last changes fastest.
Arguments:
- activations: bfloat16 [4, 1536, 4096], P('pipe', 'tensor', 'dp'), may hold values from -6 to 6
- upstream: bfloat16 [4, 1536, 4096], P('pipe', 'tensor', 'dp'), may hold values from -4 to 4
- gate_value: bfloat16 [4, 1536, 14336], P('pipe', 'dp', 'tensor'), may hold values from -6 to 6
- up_value: bfloat16 [4, 1536, 14336], P('pipe', 'dp', 'tensor'), may hold values from -6 to 6
- hidden_grad: bfloat16 [4, 1536, 14336], P('pipe', 'dp', 'tensor'), may hold values from -4 to 4
- gate_weight: bfloat16 [4, 4096, 14336], P('pipe', 'dp', 'tensor'), may hold values from -0.09375 to 0.09375
- up_weight: bfloat16 [4, 4096, 14336], P('pipe', 'dp', 'tensor'), may hold values from -0.09375 to 0.09375
- gate_mask: int32 [4, 32, 112], P('pipe', 'dp', 'tensor'), may hold values 0 or 1
- up_mask: int32 [4, 32, 112], P('pipe', 'dp', 'tensor'), may hold values 0 or 1
Outputs:
- gate_gradient: bfloat16 [4, 4096, 14336], P('pipe', 'dp', 'tensor')
- up_gradient: bfloat16 [4, 4096, 14336], P('pipe', 'dp', 'tensor')
- handed_back: bfloat16 [4, 1536, 4096], P('pipe', 'tensor', 'dp')
The draws below stay inside these ranges and needn't reach their ends.
Inputs may be any that keep to these rules, and one draw needn't show every extreme that they name: gate_mask[s, i, j] keeps (1) or prunes (0) block (i, j) of gate_weight[s]. up_mask[s, i, j] keeps (1) or prunes (0) block (i, j) of up_weight[s].
All inputs are finite; a program needn't handle non-finite values.
Results may differ from the reference program's by a relative error of at most 0.0049.
Values may be sent and summed in bfloat16 or wider, within the bound.
A program may use at most 64 MiB of HBM per device.

```python
import jax
import jax.numpy as jnp

D = 4096
FF = 14336
BLOCK = 128
TOKENS = 1536
SECTIONS = 4
N_PIPE = 4


def set_ends(array, stream_key, smallest, largest):
    shape = array.shape
    index_at = [jax.random.randint(jax.random.fold_in(stream_key, axis), (), 0, shape[axis]) for axis in range(len(shape))]
    array = array.at[tuple(index_at)].set(smallest)
    longest = shape.index(max(shape))
    index_at[longest] = (index_at[longest] + 1) % shape[longest]
    return array.at[tuple(index_at)].set(largest)


def level_of(rng, extent, pieces, low, high):
    def one(dim, shards_of):
        draws = jax.random.uniform(jax.random.fold_in(jax.random.fold_in(rng, 6), dim), (shards_of,), jnp.float32, low / len(pieces), high / len(pieces))
        return jnp.repeat(jnp.exp(draws), extent[dim] // shards_of).reshape((-1,) + (1,) * (len(extent) - dim - 1))

    gain = one(*pieces[0])
    for cut in pieces[1:]:
        gain = gain * one(*cut)
    return gain


def bell_draw(own_key, shape, scale, bound, pieces=(), kind=jnp.bfloat16):
    values = jax.random.normal(own_key, shape, jnp.float32) * scale
    if len(pieces) > 0:
        values = level_of(own_key, shape, pieces, -0.22, 0.18) * values
    return jnp.clip(values, min=-bound, max=bound).astype(kind)


def setup_inputs(seed: int = 0) -> dict:
    keys = jax.random.split(jax.random.key(seed), 10)
    activations = bell_draw(keys[0], (SECTIONS, TOKENS, D), 1.0, 6.0, ((0, 4), (1, 16), (2, 8)))
    upstream = bell_draw(keys[1], (SECTIONS, TOKENS, D), 0.25, 4.0, ((0, 4), (1, 16), (2, 8)))
    gate_value = bell_draw(keys[2], (SECTIONS, TOKENS, FF), 1.0, 6.0, ((0, 4), (1, 8), (2, 16)))
    up_value = bell_draw(keys[3], (SECTIONS, TOKENS, FF), 1.0, 6.0, ((0, 4), (1, 8), (2, 16)))
    hidden_grad = bell_draw(keys[4], (SECTIONS, TOKENS, FF), 0.25, 4.0, ((0, 4), (1, 8), (2, 16)))
    gate_weight = bell_draw(keys[5], (SECTIONS, D, FF), D ** -0.5, 0.09375, ((0, 4), (1, 8), (2, 16)))
    up_weight = bell_draw(keys[6], (SECTIONS, D, FF), D ** -0.5, 0.09375, ((0, 4), (1, 8), (2, 16)))
    gate_mask = set_ends((jax.random.randint(keys[7], (SECTIONS, D // BLOCK, FF // BLOCK), 0, 2) < 1).astype(jnp.int32), jax.random.fold_in(keys[7], 1), 0, 1)
    up_mask = set_ends((jax.random.randint(keys[8], (SECTIONS, D // BLOCK, FF // BLOCK), 0, 2) < 1).astype(jnp.int32), jax.random.fold_in(keys[8], 1), 0, 1)
    return {"activations": activations, "upstream": upstream, "gate_value": gate_value, "up_value": up_value, "hidden_grad": hidden_grad, "gate_weight": gate_weight, "up_weight": up_weight, "gate_mask": gate_mask, "up_mask": up_mask}


def apply_blocks(matrix, keep_mask):
    rows_blocks, cols_blocks = keep_mask.shape
    shaped = matrix.reshape(rows_blocks, matrix.shape[0] // rows_blocks, cols_blocks, matrix.shape[1] // cols_blocks)
    return (shaped * keep_mask.astype(matrix.dtype)[:, None, :, None]).reshape(matrix.shape)


def reference(activations, upstream, gate_value, up_value, hidden_grad, gate_weight, up_weight, gate_mask, up_mask):
    gate_list = []
    up_list = []
    sent = []
    for section in range(N_PIPE):
        gate_float = gate_value[section].astype(jnp.float32)
        up_float = up_value[section].astype(jnp.float32)
        hidden_float = hidden_grad[section].astype(jnp.float32)
        gate_sigmoid = jax.nn.sigmoid(gate_float)
        up_delta = (hidden_float * gate_float * gate_sigmoid).astype(jnp.bfloat16)
        gate_delta = (hidden_float * up_float * gate_sigmoid * (1.0 + gate_float * (1.0 - gate_sigmoid))).astype(jnp.bfloat16)
        gate_kept = apply_blocks(gate_weight[section], gate_mask[section])
        up_kept = apply_blocks(up_weight[section], up_mask[section])
        stream = activations[section]
        gate_raw = jnp.dot(stream.T, gate_delta, preferred_element_type=jnp.float32)
        up_raw = jnp.dot(stream.T, up_delta, preferred_element_type=jnp.float32)
        gate_list.append(apply_blocks(gate_raw, gate_mask[section]).astype(jnp.bfloat16))
        up_list.append(apply_blocks(up_raw, up_mask[section]).astype(jnp.bfloat16))
        branch = jnp.dot(gate_delta, gate_kept.T, preferred_element_type=jnp.float32)
        branch = branch + jnp.dot(up_delta, up_kept.T, preferred_element_type=jnp.float32)
        sent.append((upstream[section].astype(jnp.float32) + branch).astype(jnp.bfloat16))
    handed = sent[1:] + [jnp.zeros((TOKENS, D), jnp.bfloat16)]
    return jnp.stack(gate_list), jnp.stack(up_list), jnp.stack(handed)
```

```python
import jax
import jax.numpy as jnp
from jax import lax
from jax.sharding import PartitionSpec as P

PHASES = 2
F32 = jnp.float32
BF16 = jnp.bfloat16


def apply_blocks(matrix, keep_mask):
    rows_blocks, cols_blocks = keep_mask.shape
    shaped = matrix.reshape(
        rows_blocks, matrix.shape[0] // rows_blocks, cols_blocks, matrix.shape[1] // cols_blocks
    )
    return (shaped * keep_mask.astype(matrix.dtype)[:, None, :, None]).reshape(matrix.shape)


def at(array, index):
    return lax.dynamic_index_in_dim(array, index, 0, keepdims=False)


def per_device(
    activations,
    upstream,
    gate_value,
    up_value,
    hidden_grad,
    gate_weight,
    up_weight,
    gate_mask,
    up_mask,
):
    n_dp, n_tensor, n_pipe = (lax.axis_size(a) for a in ("dp", "tensor", "pipe"))
    n_x = n_tensor // 4
    j = lax.axis_index("dp")
    t = lax.axis_index("tensor")
    core, x, zh = t % 2, (t // 2) % n_x, t // (2 * n_x)

    def index(zh, x, core):
        return (zh * n_x + x) * 2 + core

    places = [(a, b, c) for a in range(2) for b in range(n_x) for c in range(2)]
    swap_core = [(index(a, b, c), index(a, b, 1 - c)) for a, b, c in places]
    swap_z = [(index(a, b, c), index(1 - a, b, c)) for a, b, c in places]

    def shift_x(s):
        return [(index(a, b, c), index(a, (b + s) % n_x, c)) for a, b, c in places]

    right = [(i, (i + 1) % n_dp) for i in range(n_dp)]
    left = [(i, (i - 1) % n_dp) for i in range(n_dp)]
    half_hops = n_dp // 2

    gate_float = gate_value[0].astype(F32)
    up_float = up_value[0].astype(F32)
    hidden_float = hidden_grad[0].astype(F32)
    gate_sigmoid = jax.nn.sigmoid(gate_float)
    up_delta = (hidden_float * gate_float * gate_sigmoid).astype(BF16)
    gate_delta = (
        hidden_float * up_float * gate_sigmoid * (1.0 + gate_float * (1.0 - gate_sigmoid))
    ).astype(BF16)
    tokens, hidden = gate_delta.shape
    width = activations.shape[2]
    rows = tokens // (2 * PHASES)
    delta = jnp.concatenate([gate_delta, up_delta], axis=1)
    delta = delta.reshape(2, PHASES, rows, 2 * hidden)

    hops = []
    for p in range(PHASES):
        own = delta[:, p].reshape(2 * rows, 2 * hidden)
        steps = [own]
        going_right = going_left = own
        for h in range(1, half_hops):
            going_right = lax.ppermute(going_right, "dp", right)
            going_left = lax.ppermute(going_left, "dp", left)
            steps.append(jnp.concatenate([going_right, going_left], axis=0))
        last_right = lax.ppermute(going_right[:rows], "dp", right)
        last_left = lax.ppermute(going_left[rows:], "dp", left)
        steps.append(jnp.concatenate([last_right, last_left], axis=0))
        hops.append(steps)

    mine = activations[0]
    pair = jnp.stack([mine, lax.ppermute(mine, "tensor", swap_z)])
    around = [pair] + [lax.ppermute(pair, "tensor", shift_x(s)) for s in range(1, n_x)]
    same_core = jnp.stack(around)
    other_core = lax.ppermute(same_core, "tensor", swap_core)
    first = jnp.where(core == 0, same_core, other_core)
    second = jnp.where(core == 0, other_core, same_core)
    stored = jnp.stack([first, second], axis=2)
    stored = stored.reshape(n_x * 2, 2, PHASES, rows, width)

    def stream_of(block):
        block_x, block_z = block % n_x, block // n_x
        place = ((x - block_x) % n_x) * 2 + (block_z + zh) % 2
        return at(stored, place)

    kept = jnp.concatenate(
        [apply_blocks(gate_weight[0], gate_mask[0]), apply_blocks(up_weight[0], up_mask[0])], axis=1
    )
    over_tokens = (((0,), (0,)), ((), ()))
    over_hidden = (((1,), (1,)), ((), ()))

    order = [0]
    for h in range(1, half_hops):
        order += [n_dp - h, h]
    order.append(half_hops)
    slot = [order.index(r) for r in range(n_dp)]

    own_rows = []
    for p in range(PHASES):
        summed = []
        for group in (hops[p][: half_hops - 1], hops[p][half_hops - 1 :]):
            parts = [
                lax.dot_general(step, kept, over_hidden, preferred_element_type=F32)
                for step in group
            ]
            part = jnp.concatenate(parts, axis=0).reshape(-1, 2, rows, width)
            here = jnp.where(core == 0, part[:, 0], part[:, 1])
            there = jnp.where(core == 0, part[:, 1], part[:, 0]).astype(BF16)
            there = lax.ppermute(there, "tensor", swap_core)
            summed.append(here + there.astype(F32))
        summed = jnp.concatenate(summed, axis=0)
        slots = jnp.array(slot, jnp.int32)

        def for_chip(chip_z, chip_x):
            return at(summed, slots[(chip_z * n_x + chip_x - j) % n_dp])

        total = jnp.stack([for_chip(a, x) for a in range(2)])
        for s in range(1, n_x):
            sent = jnp.stack([for_chip(a, (x + s) % n_x) for a in range(2)]).astype(BF16)
            total = total + lax.ppermute(sent, "tensor", shift_x(s)).astype(F32)
        away = lax.ppermute(at(total, 1 - zh).astype(BF16), "tensor", swap_z)
        own_rows.append(at(total, zh) + away.astype(F32))
    branch = jnp.concatenate(own_rows, axis=0)
    section_grad = (upstream[0].astype(F32) + branch).astype(BF16)
    handed = lax.ppermute(section_grad, "pipe", [(i, i - 1) for i in range(1, n_pipe)])

    acc = None
    for h in range(half_hops + 1):
        ids = [0] if h == 0 else [n_dp - h, h] if h < half_hops else [half_hops]
        streams = [stream_of((j + r) % n_dp) for r in ids]
        lhs = jnp.concatenate(
            [s[:, p].reshape(2 * rows, width) for p in range(PHASES) for s in streams], axis=0
        )
        rhs = jnp.concatenate([hops[p][h] for p in range(PHASES)], axis=0)
        term = lax.dot_general(lhs, rhs, over_tokens, preferred_element_type=F32)
        acc = term if acc is None else acc + term
    gate_gradient = apply_blocks(acc[:, :hidden], gate_mask[0]).astype(BF16)[None]
    up_gradient = apply_blocks(acc[:, hidden:], up_mask[0]).astype(BF16)[None]
    return (gate_gradient, up_gradient, handed[None])


def solution(mesh):
    return jax.shard_map(
        per_device,
        mesh=mesh,
        in_specs=(
            P("pipe", "tensor", "dp"),
            P("pipe", "tensor", "dp"),
            P("pipe", "dp", "tensor"),
            P("pipe", "dp", "tensor"),
            P("pipe", "dp", "tensor"),
            P("pipe", "dp", "tensor"),
            P("pipe", "dp", "tensor"),
            P("pipe", "dp", "tensor"),
            P("pipe", "dp", "tensor"),
        ),
        out_specs=(P("pipe", "dp", "tensor"), P("pipe", "dp", "tensor"), P("pipe", "tensor", "dp")),
        check_vma=False,
    )
```

```python
import jax
import jax.numpy as jnp
from jax import lax
from jax.experimental import pallas as pl
from jax.experimental.pallas import tpu as pltpu
from jax.sharding import PartitionSpec as P

F32 = jnp.float32
BF16 = jnp.bfloat16
MESH = pl.DeviceIdType.MESH
N_DP, N_X, N_PIPE = 8, 4, 4
CHIPS = 2 * N_X
HOPS = N_DP // 2
BLOCK = 128


def kernel(
    delta_ref, act_ref, up_ref, gate_w, up_w, gate_mask, up_mask,
    gate_out, up_out, handed_out,
    ring, act, act_rows, act_cols, kept, part, total,
    core_send, core_recv, x_send, x_recv, z_send, z_recv, pipe_send, pipe_recv,
    send_sem, recv_sem, local_sem,
):
    rows, hidden2 = delta_ref.shape[1:]
    hidden = hidden2 // 2
    width = act_ref.shape[1]
    j = lax.axis_index("dp")
    t = lax.axis_index("tensor")
    pipe = lax.axis_index("pipe")
    core, x, zh = t % 2, (t // 2) % N_X, t // (2 * N_X)
    chip = t // 2

    def tensor_at(z, x, c):
        return {"tensor": (z * N_X + x) * 2 + c}

    right, left = {"dp": (j + 1) % N_DP}, {"dp": (j + N_DP - 1) % N_DP}
    other_core = tensor_at(zh, x, 1 - core)
    other_z = tensor_at(1 - zh, x, core)
    along_x = [None] + [tensor_at(zh, (x + s) % N_X, core) for s in range(1, N_X)]
    before = {"pipe": (pipe + N_PIPE - 1) % N_PIPE}
    after = {"pipe": (pipe + 1) % N_PIPE}

    barrier = pltpu.get_barrier_semaphore()
    greeted = [right, left, other_core, other_z, before, after] + along_x[1:]
    for other in greeted:
        pl.semaphore_signal(barrier, inc=1, device_id=other, device_id_type=MESH)
    pl.semaphore_wait(barrier, len(greeted))

    used = [0]
    sent = []

    def copy(src, dst, target):
        k = used[0]
        used[0] += 1
        made = pltpu.make_async_remote_copy(
            src_ref=src, dst_ref=dst, send_sem=send_sem.at[k], recv_sem=recv_sem.at[k],
            device_id=target, device_id_type=MESH,
        )
        return made

    def start(made):
        made.start()
        sent.append(made)
        return made

    going = {}

    def launch(d, p, h, c):
        q = 2 * p + c
        if h == 1:
            src = delta_ref.at[q]
        else:
            src = ring.at[2 * h - 3 if d == 0 else 2 * h - 2, q]
        dst = ring.at[N_DP - 1 if h == HOPS else (2 * h - 1 if d == 0 else 2 * h), q]
        going[d, p, h, c] = start(copy(src, dst, right if d == 0 else left))

    def arrive(p, h, c):
        for d in range(2):
            going[d, p, h, c].wait_recv()
            if h < HOPS - 1:
                launch(d, p, h + 1, c)
            elif d == c:
                launch(d, p, HOPS, c)

    for c in range(2):
        for d in range(2):
            launch(d, 0, 1, c)

    act_z = start(copy(act_ref, act.at[core, chip], other_z))
    act_own = [
        start(copy(act_ref, act.at[core, chip], along_x[s])) for s in range(1, N_X)
    ]
    home = pltpu.make_async_copy(act_ref, act.at[core, chip], local_sem)
    home.start()

    ring[0] = delta_ref[...]

    def keep(k, carry):
        at = pl.multiple_of(k * BLOCK, BLOCK)
        for w, (weight, mask) in enumerate(((gate_w, gate_mask), (up_w, up_mask))):
            to = pl.multiple_of(w * hidden + k * BLOCK, BLOCK)
            for i in range(width // BLOCK):
                block = weight[i * BLOCK : (i + 1) * BLOCK, pl.ds(at, BLOCK)].astype(F32)
                block = block * mask[i, k].astype(F32)
                kept[pl.ds(to, BLOCK), i * BLOCK : (i + 1) * BLOCK] = block.T.astype(BF16)
        return carry

    lax.fori_loop(0, hidden // BLOCK, keep, 0)

    core_going = {}

    def places(h):
        return (0, 1) if h == 0 else (N_DP - 1, 1) if h == HOPS else (2 * h - 1, 2)

    def multiply(p, h):
        first, n = places(h)
        lhs = ring[first : first + n, 2 * p : 2 * p + 2].reshape(n * 2 * rows, hidden2)
        out = jnp.dot(lhs, kept[...], preferred_element_type=F32)
        part[p, first : first + n] = out.reshape(n, 2, rows, width)
        for k in range(first, first + n):
            core_send[p, k] = part[p, k, 1 - core].astype(BF16)

    def send_core(p, h):
        first, n = places(h)
        core_going[p, h] = start(
            copy(core_send.at[p, pl.ds(first, n)], core_recv.at[p, pl.ds(first, n)], other_core)
        )

    x_going, z_going, pipe_going = {}, {}, {}

    def place_of(chip_z, chip_x):
        r = (chip_z * N_X + chip_x - j + N_DP) % N_DP
        return 2 * r + (r // 4) * (15 - 4 * r)

    def reduce_core(p):
        for h in range(HOPS + 1):
            core_going[p, h].wait_recv()
        for k in range(N_DP):
            total[p, k] = part[p, k, core] + core_recv[p, k].astype(F32)
        for s in (2, 1, 3):
            for a in range(2):
                x_send[p, s - 1, a] = total[p, place_of(a, (x + s) % N_X)].astype(BF16)
        for s in (2, 1, 3):
            x_going[p, s] = start(copy(x_send.at[p, s - 1], x_recv.at[p, s - 1], along_x[s]))

    def x_sum(p, a):
        value = total[p, place_of(a, x)]
        for s in range(1, N_X):
            value = value + x_recv[p, s - 1, a].astype(F32)
        return value

    def reduce_x(p):
        for s in range(1, N_X):
            x_going[p, s].wait_recv()
        z_send[p] = x_sum(p, 1 - zh).astype(BF16)
        z_going[p] = start(copy(z_send.at[p], z_recv.at[p], other_z))

    def reduce_z(p):
        own = x_sum(p, zh)
        z_going[p].wait_recv()
        own = own + z_recv[p].astype(F32) + up_ref[p * rows : (p + 1) * rows, :].astype(F32)
        pipe_send[p] = own.astype(BF16)
        made = copy(pipe_send.at[p], pipe_recv.at[p], before)
        pipe_going[p] = made

        @pl.when(pipe > 0)
        def _():
            made.start()

    multiply(0, 0)
    send_core(0, 0)
    for h in range(1, HOPS - 1):
        for c in range(2):
            arrive(0, h, c)
        multiply(0, h)
        send_core(0, h)
        if h == 1:
            act_z.wait_recv()
            far = act.at[core, (1 - zh) * N_X + x]
            act_far = [start(copy(far, far, along_x[s])) for s in range(1, N_X)]
    arrive(0, HOPS - 1, 0)
    launch(1, 1, 1, 0)
    arrive(0, HOPS - 1, 1)
    launch(0, 1, 1, 0)
    launch(0, 1, 1, 1)
    launch(1, 1, 1, 1)
    multiply(0, HOPS - 1)
    send_core(0, HOPS - 1)
    for made in act_own + act_far:
        made.wait_recv()
    home.wait()
    act_core = start(copy(act.at[core], act.at[core], other_core))
    for d in range(2):
        going[d, 0, HOPS, d].wait_recv()
    multiply(0, HOPS)
    send_core(0, HOPS)

    multiply(1, 0)
    send_core(1, 0)
    for c in range(2):
        arrive(1, 1, c)
    reduce_core(0)
    multiply(1, 1)
    send_core(1, 1)
    for c in range(2):
        arrive(1, 2, c)
    reduce_x(0)
    multiply(1, 2)
    send_core(1, 2)
    act_core.wait_recv()
    distance = [0, 7, 1, 6, 2, 5, 3, 4]
    for k in range(N_DP):
        block = (j + distance[k]) % N_DP
        for p in range(2):
            for c in range(2):
                at = ((k * 2 + p) * 2 + c) * rows
                act_rows[at : at + rows, :] = act[c, block, p * rows : (p + 1) * rows, :]

    def turn(k, carry):
        at = pl.multiple_of(k * BLOCK, BLOCK)
        act_cols[:, pl.ds(at, BLOCK)] = act_rows[pl.ds(at, BLOCK), :].astype(F32).T.astype(BF16)
        return carry

    lax.fori_loop(0, act_rows.shape[0] // BLOCK, turn, 0)
    for c in range(2):
        arrive(1, HOPS - 1, c)
    multiply(1, HOPS - 1)
    send_core(1, HOPS - 1)
    reduce_z(0)
    for d in range(2):
        going[d, 1, HOPS, d].wait_recv()
    multiply(1, HOPS)
    send_core(1, HOPS)

    def gradient(w, at, wide, first_block):
        out, mask = ((gate_out, gate_mask), (up_out, up_mask))[w]
        rhs = ring[:, :, :, pl.ds(w * hidden + at, wide)].reshape(-1, wide)
        acc = jnp.dot(act_cols[...], rhs, preferred_element_type=F32)
        for i in range(width // BLOCK):
            for b in range(wide // BLOCK):
                block = acc[i * BLOCK : (i + 1) * BLOCK, b * BLOCK : (b + 1) * BLOCK]
                block = block * mask[i, first_block + b].astype(F32)
                out[i * BLOCK : (i + 1) * BLOCK, pl.ds(at + b * BLOCK, BLOCK)] = block.astype(BF16)

    def gradients(w):
        wide = 2 * BLOCK
        whole = hidden // wide

        def step(k, carry):
            gradient(w, pl.multiple_of(k * wide, wide), wide, 2 * k)
            return carry

        lax.fori_loop(0, whole, step, 0)
        if hidden % wide:
            gradient(w, whole * wide, BLOCK, 2 * whole)

    reduce_core(1)
    gradients(0)
    reduce_x(1)
    gradients(1)
    reduce_z(1)

    @pl.when(pipe < N_PIPE - 1)
    def _():
        for p in range(2):
            pipe_going[p].wait_recv()
            handed_out[p * rows : (p + 1) * rows, :] = pipe_recv[p]

    @pl.when(pipe == N_PIPE - 1)
    def _():
        handed_out[...] = jnp.zeros_like(handed_out)

    @pl.when(pipe > 0)
    def _():
        for p in range(2):
            pipe_going[p].wait_send()

    for made in sent:
        made.wait_send()


def per_device(
    activations, upstream, gate_value, up_value, hidden_grad,
    gate_weight, up_weight, gate_mask, up_mask,
):
    gate_float = gate_value[0].astype(F32)
    up_float = up_value[0].astype(F32)
    hidden_float = hidden_grad[0].astype(F32)
    gate_sigmoid = jax.nn.sigmoid(gate_float)
    up_delta = (hidden_float * gate_float * gate_sigmoid).astype(BF16)
    gate_delta = (
        hidden_float * up_float * gate_sigmoid * (1.0 + gate_float * (1.0 - gate_sigmoid))
    ).astype(BF16)
    tokens, hidden = gate_delta.shape
    width = activations.shape[2]
    rows = tokens // 4
    delta = jnp.concatenate([gate_delta, up_delta], axis=1)
    delta = delta.reshape(2, 2, rows, 2 * hidden).swapaxes(0, 1).reshape(4, rows, 2 * hidden)
    vmem = pl.BlockSpec(memory_space=pltpu.VMEM)
    smem = pl.BlockSpec(memory_space=pltpu.SMEM)
    copies = 64
    gate_gradient, up_gradient, handed = pl.pallas_call(
        kernel,
        out_shape=(
            jax.ShapeDtypeStruct((width, hidden), BF16),
            jax.ShapeDtypeStruct((width, hidden), BF16),
            jax.ShapeDtypeStruct((2 * rows, width), BF16),
        ),
        in_specs=[vmem] * 5 + [smem] * 2,
        out_specs=[vmem] * 3,
        scratch_shapes=[
            pltpu.VMEM((N_DP, 4, rows, 2 * hidden), BF16),
            pltpu.VMEM((2, CHIPS, 2 * rows, width), BF16),
            pltpu.VMEM((N_DP * 4 * rows, width), BF16),
            pltpu.VMEM((width, N_DP * 4 * rows), BF16),
            pltpu.VMEM((2 * hidden, width), BF16),
            pltpu.VMEM((2, N_DP, 2, rows, width), F32),
            pltpu.VMEM((2, N_DP, rows, width), F32),
            pltpu.VMEM((2, N_DP, rows, width), BF16),
            pltpu.VMEM((2, N_DP, rows, width), BF16),
            pltpu.VMEM((2, N_X - 1, 2, rows, width), BF16),
            pltpu.VMEM((2, N_X - 1, 2, rows, width), BF16),
            pltpu.VMEM((2, rows, width), BF16),
            pltpu.VMEM((2, rows, width), BF16),
            pltpu.VMEM((2, rows, width), BF16),
            pltpu.VMEM((2, rows, width), BF16),
            pltpu.SemaphoreType.DMA((copies,)),
            pltpu.SemaphoreType.DMA((copies,)),
            pltpu.SemaphoreType.DMA,
        ],
        compiler_params=pltpu.CompilerParams(
            collective_id=0, has_side_effects=True, vmem_limit_bytes=48 * 1024 * 1024
        ),
    )(
        delta, activations[0], upstream[0], gate_weight[0], up_weight[0], gate_mask[0], up_mask[0]
    )
    return (gate_gradient[None], up_gradient[None], handed[None])


def solution(mesh):
    return jax.shard_map(
        per_device,
        mesh=mesh,
        in_specs=(
            P("pipe", "tensor", "dp"),
            P("pipe", "tensor", "dp"),
            P("pipe", "dp", "tensor"),
            P("pipe", "dp", "tensor"),
            P("pipe", "dp", "tensor"),
            P("pipe", "dp", "tensor"),
            P("pipe", "dp", "tensor"),
            P("pipe", "dp", "tensor"),
            P("pipe", "dp", "tensor"),
        ),
        out_specs=(P("pipe", "dp", "tensor"), P("pipe", "dp", "tensor"), P("pipe", "tensor", "dp")),
        check_vma=False,
    )
```

```python
import jax
import jax.numpy as jnp
from jax import lax
from jax.experimental import pallas as pl
from jax.experimental.pallas import tpu as pltpu
from jax.sharding import PartitionSpec as P

F32 = jnp.float32
BF16 = jnp.bfloat16
MESH = pl.DeviceIdType.MESH
N_DP, N_X, N_PIPE = 8, 4, 4
CHIPS = 2 * N_X
HOPS = N_DP // 2
THIRDS = 3
BLOCK = 128


def kernel(
    delta_ref, act_ref, up_ref, gate_hbm, up_hbm, gate_mask, up_mask,
    gate_out, up_out, handed_out,
    ring, act, act_rows, act_cols, kept, part, total,
    core_send, core_recv, x_send, x_recv, z_send, z_recv, pipe_send, pipe_recv,
    gate_w, up_w, send_sem, recv_sem, local_sem,
):
    rows, hidden2 = delta_ref.shape[1:]
    hidden = hidden2 // 2
    width = act_ref.shape[1]
    j = lax.axis_index("dp")
    t = lax.axis_index("tensor")
    pipe = lax.axis_index("pipe")
    core, x, zh = t % 2, (t // 2) % N_X, t // (2 * N_X)
    chip = t // 2

    def tensor_at(z, x, c):
        return {"tensor": (z * N_X + x) * 2 + c}

    right, left = {"dp": (j + 1) % N_DP}, {"dp": (j + N_DP - 1) % N_DP}
    other_core = tensor_at(zh, x, 1 - core)
    other_z = tensor_at(1 - zh, x, core)
    along_x = [None] + [tensor_at(zh, (x + s) % N_X, core) for s in range(1, N_X)]
    before = {"pipe": (pipe + N_PIPE - 1) % N_PIPE}
    after = {"pipe": (pipe + 1) % N_PIPE}

    weights_in = [
        pltpu.make_async_copy(gate_hbm, gate_w, local_sem.at[1]),
        pltpu.make_async_copy(up_hbm, up_w, local_sem.at[2]),
    ]
    for made in weights_in:
        made.start()

    barrier = pltpu.get_barrier_semaphore()
    greeted = [right, left, other_core, other_z, before, after] + along_x[1:]
    for other in greeted:
        pl.semaphore_signal(barrier, inc=1, device_id=other, device_id_type=MESH)
    pl.semaphore_wait(barrier, len(greeted))

    used = [0]
    sent = []

    def copy(src, dst, target):
        k = used[0]
        used[0] += 1
        made = pltpu.make_async_remote_copy(
            src_ref=src, dst_ref=dst, send_sem=send_sem.at[k], recv_sem=recv_sem.at[k],
            device_id=target, device_id_type=MESH,
        )
        return made

    def start(made):
        made.start()
        sent.append(made)
        return made

    going = {}

    def launch(d, p, h, c):
        q = c * THIRDS + p
        if h == 1:
            src = delta_ref.at[q]
        else:
            src = ring.at[2 * h - 3 if d == 0 else 2 * h - 2, q]
        dst = ring.at[N_DP - 1 if h == HOPS else (2 * h - 1 if d == 0 else 2 * h), q]
        going[d, p, h, c] = start(copy(src, dst, right if d == 0 else left))

    def arrive(p, h, c):
        for d in range(2):
            going[d, p, h, c].wait_recv()
            if h < HOPS - 1:
                launch(d, p, h + 1, c)
            elif d == c:
                launch(d, p, HOPS, c)

    for p in range(2):
        for c in range(2):
            for d in range(2):
                launch(d, p, 1, c)

    act_z = start(copy(act_ref, act.at[core, chip], other_z))
    act_own = [
        start(copy(act_ref, act.at[core, chip], along_x[s])) for s in range(1, N_X)
    ]
    home = pltpu.make_async_copy(act_ref, act.at[core, chip], local_sem.at[0])
    home.start()

    ring[0] = delta_ref[...]

    def keep(k, carry):
        at = pl.multiple_of(k * BLOCK, BLOCK)
        for w, (weight, mask) in enumerate(((gate_w, gate_mask), (up_w, up_mask))):
            to = pl.multiple_of(w * hidden + k * BLOCK, BLOCK)
            for i in range(width // BLOCK):
                block = weight[i * BLOCK : (i + 1) * BLOCK, pl.ds(at, BLOCK)].astype(F32)
                block = block * mask[i, k].astype(F32)
                kept[pl.ds(to, BLOCK), i * BLOCK : (i + 1) * BLOCK] = block.T.astype(BF16)
        return carry

    for made in weights_in:
        made.wait()
    lax.fori_loop(0, hidden // BLOCK, keep, 0)

    core_going = {}

    def places(h):
        return (0, 1) if h == 0 else (N_DP - 1, 1) if h == HOPS else (2 * h - 1, 2)

    def multiply(p, h):
        first, n = places(h)
        lhs = jnp.concatenate(
            [
                ring[first : first + n, c * THIRDS + p].reshape(n * rows, hidden2)
                for c in range(2)
            ],
            axis=0,
        )
        out = jnp.dot(lhs, kept[...], preferred_element_type=F32)
        for c in range(2):
            part[p, first : first + n, c] = out[c * n * rows : (c + 1) * n * rows].reshape(
                n, rows, width
            )
        for k in range(first, first + n):
            core_send[p, k] = part[p, k, 1 - core].astype(BF16)

    def send_core(p, h):
        first, n = places(h)
        core_going[p, h] = start(
            copy(core_send.at[p, pl.ds(first, n)], core_recv.at[p, pl.ds(first, n)], other_core)
        )

    x_going, z_going, pipe_going = {}, {}, {}

    def place_of(chip_z, chip_x):
        r = (chip_z * N_X + chip_x - j + N_DP) % N_DP
        return 2 * r + (r // 4) * (15 - 4 * r)

    def reduce_core(p):
        for h in range(HOPS + 1):
            core_going[p, h].wait_recv()
        for k in range(N_DP):
            total[p, k] = part[p, k, core] + core_recv[p, k].astype(F32)
        for s in (2, 1, 3):
            for a in range(2):
                x_send[p, s - 1, a] = total[p, place_of(a, (x + s) % N_X)].astype(BF16)
        for s in (2, 1, 3):
            x_going[p, s] = start(copy(x_send.at[p, s - 1], x_recv.at[p, s - 1], along_x[s]))

    def x_sum(p, a):
        value = total[p, place_of(a, x)]
        for s in range(1, N_X):
            value = value + x_recv[p, s - 1, a].astype(F32)
        return value

    def reduce_x(p):
        for s in range(1, N_X):
            x_going[p, s].wait_recv()
        z_send[p] = x_sum(p, 1 - zh).astype(BF16)
        z_going[p] = start(copy(z_send.at[p], z_recv.at[p], other_z))

    def reduce_z(p):
        own = x_sum(p, zh)
        z_going[p].wait_recv()
        own = own + z_recv[p].astype(F32) + up_ref[p * rows : (p + 1) * rows, :].astype(F32)
        pipe_send[p] = own.astype(BF16)
        made = copy(pipe_send.at[p], pipe_recv.at[p], before)
        pipe_going[p] = made

        @pl.when(pipe > 0)
        def _():
            made.start()

    def turn(k, carry):
        at = pl.multiple_of(k * BLOCK, BLOCK)
        act_cols[:, pl.ds(at, BLOCK)] = act_rows[pl.ds(at, BLOCK), :].astype(F32).T.astype(BF16)
        return carry

    def order_rows():
        distance = [0, 7, 1, 6, 2, 5, 3, 4]
        for k in range(N_DP):
            block = (j + distance[k]) % N_DP
            for c in range(2):
                at = (k * 2 + c) * THIRDS * rows
                act_rows[at : at + THIRDS * rows, :] = act[c, block]
        lax.fori_loop(0, act_rows.shape[0] // BLOCK, turn, 0)

    for p in range(2):
        multiply(p, 0)
        send_core(p, 0)
    for h in range(1, HOPS - 1):
        for p in range(2):
            for c in range(2):
                arrive(p, h, c)
        if h == 1:
            act_z.wait_recv()
            far = act.at[core, (1 - zh) * N_X + x]
            act_far = [start(copy(far, far, along_x[s])) for s in range(1, N_X)]
        for p in range(2):
            multiply(p, h)
            send_core(p, h)
    for made in act_own + act_far:
        made.wait_recv()
    home.wait()
    act_core = start(copy(act.at[core], act.at[core], other_core))
    for c in range(2):
        arrive(0, HOPS - 1, c)
    for d in range(2):
        launch(d, 2, 1, 0)
    arrive(1, HOPS - 1, 0)
    for d in range(2):
        launch(d, 2, 1, 1)
    arrive(1, HOPS - 1, 1)
    act_core.wait_recv()
    order_rows()
    for p in range(2):
        multiply(p, HOPS - 1)
        send_core(p, HOPS - 1)

    for d in range(2):
        going[d, 0, HOPS, d].wait_recv()
    multiply(0, HOPS)
    send_core(0, HOPS)
    arrive(2, 1, 0)
    arrive(2, 1, 1)
    for d in range(2):
        going[d, 1, HOPS, d].wait_recv()
    multiply(1, HOPS)
    send_core(1, HOPS)
    reduce_core(0)
    arrive(2, 2, 0)
    reduce_core(1)
    arrive(2, 2, 1)
    multiply(2, 0)
    send_core(2, 0)
    multiply(2, 1)
    send_core(2, 1)
    arrive(2, HOPS - 1, 0)
    reduce_x(0)
    arrive(2, HOPS - 1, 1)
    reduce_x(1)
    multiply(2, 2)
    send_core(2, 2)
    multiply(2, HOPS - 1)
    send_core(2, HOPS - 1)
    for d in range(2):
        going[d, 2, HOPS, d].wait_recv()
    multiply(2, HOPS)
    send_core(2, HOPS)

    def gradient(w, at, wide, first_block):
        out, mask = ((gate_out, gate_mask), (up_out, up_mask))[w]
        rhs = ring[:, :, :, pl.ds(w * hidden + at, wide)].reshape(-1, wide)
        acc = jnp.dot(act_cols[...], rhs, preferred_element_type=F32)
        for i in range(width // BLOCK):
            for b in range(wide // BLOCK):
                block = acc[i * BLOCK : (i + 1) * BLOCK, b * BLOCK : (b + 1) * BLOCK]
                block = block * mask[i, first_block + b].astype(F32)
                out[i * BLOCK : (i + 1) * BLOCK, pl.ds(at + b * BLOCK, BLOCK)] = block.astype(BF16)

    def gradients(w):
        wide = 2 * BLOCK
        whole = hidden // wide

        def step(k, carry):
            gradient(w, pl.multiple_of(k * wide, wide), wide, 2 * k)
            return carry

        lax.fori_loop(0, whole, step, 0)
        if hidden % wide:
            gradient(w, whole * wide, BLOCK, 2 * whole)

    reduce_core(2)
    reduce_z(0)
    reduce_z(1)
    gradients(0)
    reduce_x(2)
    gradients(1)
    reduce_z(2)

    @pl.when(pipe < N_PIPE - 1)
    def _():
        for p in range(THIRDS):
            pipe_going[p].wait_recv()
            handed_out[p * rows : (p + 1) * rows, :] = pipe_recv[p]

    @pl.when(pipe == N_PIPE - 1)
    def _():
        handed_out[...] = jnp.zeros_like(handed_out)

    @pl.when(pipe > 0)
    def _():
        for p in range(THIRDS):
            pipe_going[p].wait_send()

    for made in sent:
        made.wait_send()


def per_device(
    activations, upstream, gate_value, up_value, hidden_grad,
    gate_weight, up_weight, gate_mask, up_mask,
):
    gate_float = gate_value[0].astype(F32)
    up_float = up_value[0].astype(F32)
    hidden_float = hidden_grad[0].astype(F32)
    gate_sigmoid = jax.nn.sigmoid(gate_float)
    up_delta = (hidden_float * gate_float * gate_sigmoid).astype(BF16)
    gate_delta = (
        hidden_float * up_float * gate_sigmoid * (1.0 + gate_float * (1.0 - gate_sigmoid))
    ).astype(BF16)
    tokens, hidden = gate_delta.shape
    width = activations.shape[2]
    rows = tokens // (2 * THIRDS)
    delta = jnp.concatenate([gate_delta, up_delta], axis=1)
    delta = delta.reshape(2 * THIRDS, rows, 2 * hidden)
    vmem = pl.BlockSpec(memory_space=pltpu.VMEM)
    smem = pl.BlockSpec(memory_space=pltpu.SMEM)
    copies = 80
    gate_gradient, up_gradient, handed = pl.pallas_call(
        kernel,
        out_shape=(
            jax.ShapeDtypeStruct((width, hidden), BF16),
            jax.ShapeDtypeStruct((width, hidden), BF16),
            jax.ShapeDtypeStruct((THIRDS * rows, width), BF16),
        ),
        in_specs=[vmem] * 3 + [pl.BlockSpec(memory_space=pltpu.HBM)] * 2 + [smem] * 2,
        out_specs=[vmem] * 3,
        scratch_shapes=[
            pltpu.VMEM((N_DP, 2 * THIRDS, rows, 2 * hidden), BF16),
            pltpu.VMEM((2, CHIPS, THIRDS * rows, width), BF16),
            pltpu.VMEM((N_DP * 2 * THIRDS * rows, width), BF16),
            pltpu.VMEM((width, N_DP * 2 * THIRDS * rows), BF16),
            pltpu.VMEM((2 * hidden, width), BF16),
            pltpu.VMEM((THIRDS, N_DP, 2, rows, width), F32),
            pltpu.VMEM((THIRDS, N_DP, rows, width), F32),
            pltpu.VMEM((THIRDS, N_DP, rows, width), BF16),
            pltpu.VMEM((THIRDS, N_DP, rows, width), BF16),
            pltpu.VMEM((THIRDS, N_X - 1, 2, rows, width), BF16),
            pltpu.VMEM((THIRDS, N_X - 1, 2, rows, width), BF16),
            pltpu.VMEM((THIRDS, rows, width), BF16),
            pltpu.VMEM((THIRDS, rows, width), BF16),
            pltpu.VMEM((THIRDS, rows, width), BF16),
            pltpu.VMEM((THIRDS, rows, width), BF16),
            pltpu.VMEM((width, hidden), BF16),
            pltpu.VMEM((width, hidden), BF16),
            pltpu.SemaphoreType.DMA((copies,)),
            pltpu.SemaphoreType.DMA((copies,)),
            pltpu.SemaphoreType.DMA((3,)),
        ],
        compiler_params=pltpu.CompilerParams(
            collective_id=0, has_side_effects=True, vmem_limit_bytes=40 * 1024 * 1024
        ),
    )(
        delta, activations[0], upstream[0], gate_weight[0], up_weight[0], gate_mask[0], up_mask[0]
    )
    return (gate_gradient[None], up_gradient[None], handed[None])


def solution(mesh):
    return jax.shard_map(
        per_device,
        mesh=mesh,
        in_specs=(
            P("pipe", "tensor", "dp"),
            P("pipe", "tensor", "dp"),
            P("pipe", "dp", "tensor"),
            P("pipe", "dp", "tensor"),
            P("pipe", "dp", "tensor"),
            P("pipe", "dp", "tensor"),
            P("pipe", "dp", "tensor"),
            P("pipe", "dp", "tensor"),
            P("pipe", "dp", "tensor"),
        ),
        out_specs=(P("pipe", "dp", "tensor"), P("pipe", "dp", "tensor"), P("pipe", "tensor", "dp")),
        check_vma=False,
    )
```

```python
import jax
import jax.numpy as jnp
from jax import lax
from jax.experimental import pallas as pl
from jax.experimental.pallas import tpu as pltpu
from jax.sharding import PartitionSpec as P

F32 = jnp.float32
BF16 = jnp.bfloat16
MESH = pl.DeviceIdType.MESH
N_DP, N_X, N_PIPE = 8, 4, 4
CHIPS = 2 * N_X
HOPS = N_DP // 2
THIRDS = 3
BLOCK = 128


def kernel(
    delta_ref, act_ref, up_ref, gate_hbm, up_hbm, gate_mask, up_mask,
    gate_out, up_out, handed_out,
    ring, act, act_rows, act_cols, kept, part, total,
    core_send, core_recv, x_send, x_recv, z_send, z_recv, pipe_send, pipe_recv,
    gate_w, up_w, send_sem, recv_sem, local_sem,
):
    rows, hidden2 = delta_ref.shape[1:]
    hidden = hidden2 // 2
    width = act_ref.shape[1]
    j = lax.axis_index("dp")
    t = lax.axis_index("tensor")
    pipe = lax.axis_index("pipe")
    core, x, zh = t % 2, (t // 2) % N_X, t // (2 * N_X)
    chip = t // 2

    def tensor_at(z, x, c):
        return {"tensor": (z * N_X + x) * 2 + c}

    right, left = {"dp": (j + 1) % N_DP}, {"dp": (j + N_DP - 1) % N_DP}
    other_core = tensor_at(zh, x, 1 - core)
    other_z = tensor_at(1 - zh, x, core)
    along_x = [None] + [tensor_at(zh, (x + s) % N_X, core) for s in range(1, N_X)]
    before = {"pipe": (pipe + N_PIPE - 1) % N_PIPE}
    after = {"pipe": (pipe + 1) % N_PIPE}

    weights_in = [
        pltpu.make_async_copy(gate_hbm, gate_w, local_sem.at[1]),
        pltpu.make_async_copy(up_hbm, up_w, local_sem.at[2]),
    ]
    for made in weights_in:
        made.start()

    barrier = pltpu.get_barrier_semaphore()
    greeted = [right, left, other_core, other_z, before, after] + along_x[1:]
    for other in greeted:
        pl.semaphore_signal(barrier, inc=1, device_id=other, device_id_type=MESH)
    pl.semaphore_wait(barrier, len(greeted))

    used = [0]
    sent = []

    def copy(src, dst, target):
        k = used[0]
        used[0] += 1
        made = pltpu.make_async_remote_copy(
            src_ref=src, dst_ref=dst, send_sem=send_sem.at[k], recv_sem=recv_sem.at[k],
            device_id=target, device_id_type=MESH,
        )
        return made

    def start(made):
        made.start()
        sent.append(made)
        return made

    going = {}

    def launch(d, p, h, c):
        q = c * THIRDS + p
        if h == 1:
            src = delta_ref.at[q]
        else:
            src = ring.at[2 * h - 3 if d == 0 else 2 * h - 2, q]
        dst = ring.at[N_DP - 1 if h == HOPS else (2 * h - 1 if d == 0 else 2 * h), q]
        going[d, p, h, c] = start(copy(src, dst, right if d == 0 else left))

    def arrive(p, h, c):
        for d in range(2):
            going[d, p, h, c].wait_recv()
            if h < HOPS - 1:
                launch(d, p, h + 1, c)
            elif d == c:
                launch(d, p, HOPS, c)

    for p in range(2):
        for c in range(2):
            for d in range(2):
                launch(d, p, 1, c)

    act_z = start(copy(act_ref, act.at[core, chip], other_z))
    act_own = [
        start(copy(act_ref, act.at[core, chip], along_x[s])) for s in range(1, N_X)
    ]
    home = pltpu.make_async_copy(act_ref, act.at[core, chip], local_sem.at[0])
    home.start()

    ring[0] = delta_ref[...]

    def keep(k, carry):
        at = pl.multiple_of(k * BLOCK, BLOCK)
        for w, (weight, mask) in enumerate(((gate_w, gate_mask), (up_w, up_mask))):
            to = pl.multiple_of(w * hidden + k * BLOCK, BLOCK)
            for i in range(width // BLOCK):
                block = weight[i * BLOCK : (i + 1) * BLOCK, pl.ds(at, BLOCK)].astype(F32)
                block = block * mask[i, k].astype(F32)
                kept[pl.ds(to, BLOCK), i * BLOCK : (i + 1) * BLOCK] = block.T.astype(BF16)
        return carry

    for made in weights_in:
        made.wait()
    lax.fori_loop(0, hidden // BLOCK, keep, 0)

    core_going = {}

    def places(h):
        return (0, 1) if h == 0 else (N_DP - 1, 1) if h == HOPS else (2 * h - 1, 2)

    def multiply(p, h):
        first, n = places(h)
        lhs = jnp.concatenate(
            [
                ring[first : first + n, c * THIRDS + p].reshape(n * rows, hidden2)
                for c in range(2)
            ],
            axis=0,
        )
        out = jnp.dot(lhs, kept[...], preferred_element_type=F32)
        for c in range(2):
            part[p, first : first + n, c] = out[c * n * rows : (c + 1) * n * rows].reshape(
                n, rows, width
            )
        for k in range(first, first + n):
            core_send[p, k] = part[p, k, 1 - core].astype(BF16)

    def send_core(p, h):
        first, n = places(h)
        core_going[p, h] = start(
            copy(core_send.at[p, pl.ds(first, n)], core_recv.at[p, pl.ds(first, n)], other_core)
        )

    x_going, z_going, pipe_going = {}, {}, {}

    def place_of(chip_z, chip_x):
        r = (chip_z * N_X + chip_x - j + N_DP) % N_DP
        return 2 * r + (r // 4) * (15 - 4 * r)

    def reduce_core(p):
        for h in range(HOPS + 1):
            core_going[p, h].wait_recv()
        for k in range(N_DP):
            total[p, k] = part[p, k, core] + core_recv[p, k].astype(F32)
        for s in (2, 1, 3):
            for a in range(2):
                x_send[p, s - 1, a] = total[p, place_of(a, (x + s) % N_X)].astype(BF16)
        for s in (2, 1, 3):
            x_going[p, s] = start(copy(x_send.at[p, s - 1], x_recv.at[p, s - 1], along_x[s]))

    def x_sum(p, a):
        value = total[p, place_of(a, x)]
        for s in range(1, N_X):
            value = value + x_recv[p, s - 1, a].astype(F32)
        return value

    def reduce_x(p):
        for s in range(1, N_X):
            x_going[p, s].wait_recv()
        z_send[p] = x_sum(p, 1 - zh).astype(BF16)
        z_going[p] = start(copy(z_send.at[p], z_recv.at[p], other_z))

    def reduce_z(p):
        own = x_sum(p, zh)
        z_going[p].wait_recv()
        own = own + z_recv[p].astype(F32) + up_ref[p * rows : (p + 1) * rows, :].astype(F32)
        pipe_send[p] = own.astype(BF16)
        made = copy(pipe_send.at[p], pipe_recv.at[p], before)
        pipe_going[p] = made

        @pl.when(pipe > 0)
        def _():
            made.start()

    def turn(k, carry):
        at = pl.multiple_of(k * BLOCK, BLOCK)
        act_cols[:, pl.ds(at, BLOCK)] = act_rows[pl.ds(at, BLOCK), :].astype(F32).T.astype(BF16)
        return carry

    def order_rows():
        distance = [0, 7, 1, 6, 2, 5, 3, 4]
        for k in range(N_DP):
            block = (j + distance[k]) % N_DP
            for c in range(2):
                at = (k * 2 + c) * THIRDS * rows
                act_rows[at : at + THIRDS * rows, :] = act[c, block]
        lax.fori_loop(0, act_rows.shape[0] // BLOCK, turn, 0)

    for p in range(2):
        multiply(p, 0)
        send_core(p, 0)
    for h in range(1, HOPS - 1):
        for p in range(2):
            for c in range(2):
                arrive(p, h, c)
        if h == 1:
            act_z.wait_recv()
            far = act.at[core, (1 - zh) * N_X + x]
            act_far = [start(copy(far, far, along_x[s])) for s in range(1, N_X)]
        for p in range(2):
            multiply(p, h)
            send_core(p, h)
    for made in act_own + act_far:
        made.wait_recv()
    home.wait()
    act_core = start(copy(act.at[core], act.at[core], other_core))
    for c in range(2):
        arrive(0, HOPS - 1, c)
    for d in range(2):
        launch(d, 2, 1, 0)
    arrive(1, HOPS - 1, 0)
    for d in range(2):
        launch(d, 2, 1, 1)
    arrive(1, HOPS - 1, 1)
    act_core.wait_recv()
    order_rows()
    for p in range(2):
        multiply(p, HOPS - 1)
        send_core(p, HOPS - 1)

    for d in range(2):
        going[d, 0, HOPS, d].wait_recv()
    multiply(0, HOPS)
    send_core(0, HOPS)
    arrive(2, 1, 0)
    arrive(2, 1, 1)
    for d in range(2):
        going[d, 1, HOPS, d].wait_recv()
    multiply(1, HOPS)
    send_core(1, HOPS)
    reduce_core(0)
    arrive(2, 2, 0)
    reduce_core(1)
    arrive(2, 2, 1)
    multiply(2, 0)
    send_core(2, 0)
    multiply(2, 1)
    send_core(2, 1)
    arrive(2, HOPS - 1, 0)
    reduce_x(0)
    arrive(2, HOPS - 1, 1)
    reduce_x(1)
    multiply(2, 2)
    send_core(2, 2)
    multiply(2, HOPS - 1)
    send_core(2, HOPS - 1)
    for d in range(2):
        going[d, 2, HOPS, d].wait_recv()
    multiply(2, HOPS)
    send_core(2, HOPS)

    def gradient(w, at, wide, first_block):
        out, mask = ((gate_out, gate_mask), (up_out, up_mask))[w]
        rhs = ring[:, :, :, pl.ds(w * hidden + at, wide)].reshape(-1, wide)
        acc = jnp.dot(act_cols[...], rhs, preferred_element_type=F32)
        for i in range(width // BLOCK):
            for b in range(wide // BLOCK):
                block = acc[i * BLOCK : (i + 1) * BLOCK, b * BLOCK : (b + 1) * BLOCK]
                block = block * mask[i, first_block + b].astype(F32)
                out[i * BLOCK : (i + 1) * BLOCK, pl.ds(at + b * BLOCK, BLOCK)] = block.astype(BF16)

    def gradients(w):
        wide = 2 * BLOCK
        whole = hidden // wide

        def step(k, carry):
            gradient(w, pl.multiple_of(k * wide, wide), wide, 2 * k)
            return carry

        lax.fori_loop(0, whole, step, 0)
        if hidden % wide:
            gradient(w, whole * wide, BLOCK, 2 * whole)

    reduce_core(2)
    reduce_z(0)
    reduce_z(1)
    gradients(0)
    reduce_x(2)
    gradients(1)
    reduce_z(2)

    @pl.when(pipe < N_PIPE - 1)
    def _():
        for p in range(THIRDS):
            pipe_going[p].wait_recv()
            handed_out[p * rows : (p + 1) * rows, :] = pipe_recv[p]

    @pl.when(pipe == N_PIPE - 1)
    def _():
        handed_out[...] = jnp.zeros_like(handed_out)

    @pl.when(pipe > 0)
    def _():
        for p in range(THIRDS):
            pipe_going[p].wait_send()

    for made in sent:
        made.wait_send()


def per_device(
    activations, upstream, gate_value, up_value, hidden_grad,
    gate_weight, up_weight, gate_mask, up_mask,
):
    gate_float = gate_value[0].astype(F32)
    up_float = up_value[0].astype(F32)
    hidden_float = hidden_grad[0].astype(F32)
    gate_sigmoid = jax.nn.sigmoid(gate_float)
    up_delta = (hidden_float * gate_float * gate_sigmoid).astype(BF16)
    gate_delta = (
        hidden_float * up_float * gate_sigmoid * (1.0 + gate_float * (1.0 - gate_sigmoid))
    ).astype(BF16)
    tokens, hidden = gate_delta.shape
    width = activations.shape[2]
    rows = tokens // (2 * THIRDS)
    delta = jnp.concatenate([gate_delta, up_delta], axis=1)
    delta = delta.reshape(2 * THIRDS, rows, 2 * hidden)
    vmem = pl.BlockSpec(memory_space=pltpu.VMEM)
    smem = pl.BlockSpec(memory_space=pltpu.SMEM)
    copies = 80
    gate_gradient, up_gradient, handed = pl.pallas_call(
        kernel,
        out_shape=(
            jax.ShapeDtypeStruct((width, hidden), BF16),
            jax.ShapeDtypeStruct((width, hidden), BF16),
            jax.ShapeDtypeStruct((THIRDS * rows, width), BF16),
        ),
        in_specs=[vmem] * 3 + [pl.BlockSpec(memory_space=pltpu.HBM)] * 2 + [smem] * 2,
        out_specs=[vmem] * 3,
        scratch_shapes=[
            pltpu.VMEM((N_DP, 2 * THIRDS, rows, 2 * hidden), BF16),
            pltpu.VMEM((2, CHIPS, THIRDS * rows, width), BF16),
            pltpu.VMEM((N_DP * 2 * THIRDS * rows, width), BF16),
            pltpu.VMEM((width, N_DP * 2 * THIRDS * rows), BF16),
            pltpu.VMEM((2 * hidden, width), BF16),
            pltpu.VMEM((THIRDS, N_DP, 2, rows, width), F32),
            pltpu.VMEM((THIRDS, N_DP, rows, width), F32),
            pltpu.VMEM((THIRDS, N_DP, rows, width), BF16),
            pltpu.VMEM((THIRDS, N_DP, rows, width), BF16),
            pltpu.VMEM((THIRDS, N_X - 1, 2, rows, width), BF16),
            pltpu.VMEM((THIRDS, N_X - 1, 2, rows, width), BF16),
            pltpu.VMEM((THIRDS, rows, width), BF16),
            pltpu.VMEM((THIRDS, rows, width), BF16),
            pltpu.VMEM((THIRDS, rows, width), BF16),
            pltpu.VMEM((THIRDS, rows, width), BF16),
            pltpu.VMEM((width, hidden), BF16),
            pltpu.VMEM((width, hidden), BF16),
            pltpu.SemaphoreType.DMA((copies,)),
            pltpu.SemaphoreType.DMA((copies,)),
            pltpu.SemaphoreType.DMA((3,)),
        ],
        compiler_params=pltpu.CompilerParams(
            collective_id=0, has_side_effects=True, vmem_limit_bytes=51 * 1024 * 1024
        ),
    )(
        delta, activations[0], upstream[0], gate_weight[0], up_weight[0], gate_mask[0], up_mask[0]
    )
    return (gate_gradient[None], up_gradient[None], handed[None])


def solution(mesh):
    return jax.shard_map(
        per_device,
        mesh=mesh,
        in_specs=(
            P("pipe", "tensor", "dp"),
            P("pipe", "tensor", "dp"),
            P("pipe", "dp", "tensor"),
            P("pipe", "dp", "tensor"),
            P("pipe", "dp", "tensor"),
            P("pipe", "dp", "tensor"),
            P("pipe", "dp", "tensor"),
            P("pipe", "dp", "tensor"),
            P("pipe", "dp", "tensor"),
        ),
        out_specs=(P("pipe", "dp", "tensor"), P("pipe", "dp", "tensor"), P("pipe", "tensor", "dp")),
        check_vma=False,
    )
```
